32 devices in a mesh: sys: 8 (over z, core), graph: 4 (over y, x).
Axes of the slice: x: 2, y: 2, z: 4, core: 2. Of those that a mesh axis runs over, the one named last changes fastest.
Arguments:
- node_features: bfloat16 [8, 64, 25, 128], P('sys', 'graph'), may hold values from -6 to 6
- atom_slot: int32 [8, 64], P('sys'), may hold values from 0 to 63, each once within a row
- neighbour: int32 [8, 4608], P('sys', 'graph'), may hold values from 0 to 63
- pad_mask: int32 [8, 4608], P('sys', 'graph'), may hold values 0 or 1
- envelope: float32 [8, 4608], P('sys', 'graph'), may hold values from 0.1 to 1
- wigner_rows: bfloat16 [8, 13, 25, 4608], P('sys', None, None, 'graph'), may hold values from -1.1953125 to 1.1953125
- mix_table: float32 [8, 8], replicated, may hold values from 0.1 to 2
- zero_weight: bfloat16 [8, 640, 640], P('sys', 'graph'), may hold values from -0.078125 to 0.078125
- one_weight: bfloat16 [8, 512, 2, 512], P('sys', 'graph'), may hold values from -0.0625 to 0.0625
Outputs:
- update: bfloat16 [8, 64, 25, 128], P('sys', 'graph')
The draws below stay inside these ranges and needn't reach their ends.
Inputs may be any that keep to these rules, and one draw needn't show every extreme that they name: `neighbour`: atom ids of the edge's own system; edge slots a * 72 to a * 72 + 71 belong to the atom in row a of node_features. `atom_slot`: each system's row names every row of node_features once.
All inputs are finite; a program needn't handle non-finite values. No bound on the sum of `pad_mask` on one device may be relied on, other than what follows from the above.
Results may differ from the reference program's by a relative error of at most 0.025.
Values may be sent and summed in bfloat16 or wider, within the bound.
A program may use at most 64 MiB of HBM per device.

```python
import math
import jax
import jax.numpy as jnp
from jax import lax

C = 128
LMAX = 4
NEIGH = 72
SH = 25
FRAME = 13
M0 = 640
M1 = 512
EXPERTS = 8
SYSTEMS = 8
ATOMS = 64
EDGES = 4608


def touch_ends(entries, own_key, low, top_value):
    spot = [jax.random.randint(jax.random.fold_in(own_key, axis), (), 0, length) for axis, length in enumerate(entries.shape)]
    widest = entries.shape.index(max(entries.shape))
    beside = spot[:widest] + [(spot[widest] + 1) % entries.shape[widest]] + spot[widest + 1:]
    return entries.at[tuple(spot)].set(low).at[tuple(beside)].set(top_value)


def shard_levels(stream_key, dims, shards, smallest, high):
    def one(axis_at, parts):
        heights = jax.random.uniform(jax.random.fold_in(jax.random.fold_in(stream_key, 6), axis_at), (parts,), jnp.float32, smallest / len(shards), high / len(shards))
        return jnp.repeat(jnp.exp(heights), dims[axis_at] // parts).reshape((-1,) + (1,) * (len(dims) - axis_at - 1))

    loudness = one(*shards[0])
    for cut in shards[1:]:
        loudness = loudness * one(*cut)
    return loudness


def gaussian(key, shape, deviation, bound, split=(), held_as=jnp.bfloat16):
    loudness = shard_levels(key, shape, split, -0.22, 0.18) if split else 1.0
    array = jax.random.normal(key, shape, jnp.float32) * deviation * loudness
    return jnp.minimum(jnp.maximum(array, -bound), bound).astype(held_as)


def setup_inputs(seed: int = 0) -> dict:
    arg_keys = jax.random.split(jax.random.key(seed), 10)
    return {
        "node_features": gaussian(arg_keys[0], (SYSTEMS, ATOMS, SH, C), 1.0, 6.0, ((0, 8), (1, 4))),
        "atom_slot": jax.vmap(lambda own: jax.random.permutation(own, ATOMS))(jax.random.split(arg_keys[1], SYSTEMS)).reshape((SYSTEMS, ATOMS)).astype(jnp.int32),
        "neighbour": touch_ends(jax.random.randint(arg_keys[2], (SYSTEMS, EDGES), 0, ATOMS), jax.random.fold_in(arg_keys[2], 1), 0, ATOMS - 1).astype(jnp.int32),
        "pad_mask": touch_ends((jax.random.randint(arg_keys[3], (SYSTEMS, EDGES), 0, 8) < 7).astype(jnp.int32), jax.random.fold_in(arg_keys[3], 1), 0, 1),
        "envelope": jnp.clip(jnp.exp(math.log(1.0) - 2.3025851 * jax.random.uniform(arg_keys[4], (SYSTEMS, EDGES), jnp.float32) ** shard_levels(arg_keys[4], (SYSTEMS, EDGES), ((0, 8), (1, 4)), -0.2, 0.2)), 0.1, 1.0),
        "wigner_rows": gaussian(arg_keys[5], (SYSTEMS, FRAME, SH, EDGES), 0.2, 1.1953125, ((0, 8), (3, 4))),
        "mix_table": jnp.clip(jnp.exp(jax.random.uniform(arg_keys[6], (SYSTEMS, EXPERTS), jnp.float32, math.log(0.1), math.log(2.0))), 0.1, 2.0),
        "zero_weight": gaussian(arg_keys[7], (EXPERTS, M0, M0), (M0 * EXPERTS) ** -0.5, 0.078125, ((0, 8), (1, 4))),
        "one_weight": gaussian(arg_keys[8], (EXPERTS, M1, 2, M1), (2 * M1 * EXPERTS) ** -0.5, 0.0625, ((0, 8), (1, 4))),
    }


def scaled_term(factor, weight):
    term = (factor * weight.astype(jnp.float32)).astype(jnp.bfloat16)
    term = lax.optimization_barrier(term)
    return term.astype(jnp.float32)

def one_system(inputs):
    features, slots, neighbour, pad_mask, envelope, wigner, merged_zero, merged_one = inputs
    source = jnp.take(slots, neighbour, axis=0)
    gathered = jnp.take(features, source, axis=0)
    rotated = jnp.einsum('rke,ekc->erc', wigner.astype(jnp.float32), gathered.astype(jnp.float32)).astype(jnp.bfloat16)
    edge_count = rotated.shape[0]
    channels = rotated.shape[2]
    first = rotated[:, :LMAX + 1].reshape(edge_count, -1)
    plus_part = rotated[:, LMAX + 1:2 * LMAX + 1].reshape(edge_count, -1)
    minus_part = rotated[:, 2 * LMAX + 1:].reshape(edge_count, -1)
    edge_gate = envelope * pad_mask.astype(jnp.float32)
    real_part = merged_one[:, 0, :]
    imag_part = merged_one[:, 1, :]
    out_zero = jnp.dot(first, merged_zero.T, preferred_element_type=jnp.float32)
    out_plus = jnp.dot(plus_part, real_part.T, preferred_element_type=jnp.float32) - jnp.dot(minus_part, imag_part.T, preferred_element_type=jnp.float32)
    out_minus = jnp.dot(plus_part, imag_part.T, preferred_element_type=jnp.float32) + jnp.dot(minus_part, real_part.T, preferred_element_type=jnp.float32)
    out_zero = (edge_gate[:, None] * out_zero).astype(jnp.bfloat16)
    out_plus = (edge_gate[:, None] * out_plus).astype(jnp.bfloat16)
    out_minus = (edge_gate[:, None] * out_minus).astype(jnp.bfloat16)
    message = jnp.concatenate([out_zero.reshape(edge_count, LMAX + 1, channels), out_plus.reshape(edge_count, LMAX, channels), out_minus.reshape(edge_count, LMAX, channels)], axis=1)
    atom_count = edge_count // NEIGH
    total = jnp.einsum('rkaj,ajrc->akc', wigner.astype(jnp.float32).reshape(wigner.shape[0], wigner.shape[1], atom_count, NEIGH), message.astype(jnp.float32).reshape(atom_count, NEIGH, message.shape[1], channels))
    return (total * (1.0 / math.sqrt(NEIGH))).astype(jnp.bfloat16)

def reference(node_features, atom_slot, neighbour, pad_mask, envelope, wigner_rows, mix_table, zero_weight, one_weight):
    systems = mix_table.shape[0]

    def add_expert(totals, inputs):
        weight_zero, weight_one, column = inputs
        total_zero, total_one = totals
        total_zero = total_zero + scaled_term(column[:, None, None], weight_zero[None])
        total_one = total_one + scaled_term(column[:, None, None, None], weight_one[None])
        return ((total_zero, total_one), None)
    start = (jnp.zeros((systems,) + zero_weight.shape[1:], jnp.float32), jnp.zeros((systems,) + one_weight.shape[1:], jnp.float32))
    (merged_zero, merged_one), _ = lax.scan(add_expert, start, (zero_weight, one_weight, mix_table.T))
    merged_zero = merged_zero.astype(jnp.bfloat16)
    merged_one = merged_one.astype(jnp.bfloat16)
    return lax.map(one_system, (node_features, atom_slot, neighbour, pad_mask, envelope, wigner_rows, merged_zero, merged_one))
```

```python
import functools
import math

import jax
import jax.numpy as jnp
from jax import lax
from jax.experimental import pallas as pl
from jax.experimental.pallas import tpu as pltpu
from jax.sharding import PartitionSpec as P

LMAX = 4
NEIGH = 72
CORES = 2
LANES = 128
WIDE = 256
HALVES = 2
MESH = pl.DeviceIdType.MESH


def tree_sum(terms):
    while len(terms) > 1:
        terms = [
            terms[i] + terms[i + 1] if i + 1 < len(terms) else terms[i]
            for i in range(0, len(terms), 2)
        ]
    return terms[0]


def kernel(
    chips,
    peers,
    feat_ref,
    slot_ref,
    near_ref,
    gate_ref,
    frame_ref,
    mix_ref,
    zero_ref,
    one_ref,
    out_ref,
    feats,
    turned,
    chosen,
    picked,
    rows32,
    spread,
    rotated,
    message,
    padded,
    raw_zero,
    raw_one,
    part_zero,
    part_one,
    end_zero,
    end_one,
    map_zero,
    map_one,
    stacked,
    total,
    raw_send,
    raw_recv,
    part_send,
    part_recv,
    feat_send,
    feat_recv,
    map_send,
    map_recv,
):
    experts = chips * CORES
    sys_index = lax.axis_index("sys")
    graph_index = lax.axis_index("graph")
    chip = sys_index // CORES
    core = sys_index % CORES
    up_id = jnp.minimum(sys_index + CORES, experts - 1)
    down_id = jnp.maximum(sys_index - CORES, 0)
    partner_id = chip * CORES + (1 - core)
    last = chips - 1
    is_inner = jnp.logical_and(chip > 0, chip < last)
    is_end = jnp.logical_or(chip == 0, chip == last)

    barrier = pltpu.get_barrier_semaphore()

    def greet(target_sys, target_graph):
        pl.semaphore_signal(
            barrier, inc=1, device_id=(target_sys, target_graph), device_id_type=MESH
        )

    @pl.when(chip < last)
    def _():
        greet(up_id, graph_index)

    @pl.when(chip > 0)
    def _():
        greet(down_id, graph_index)

    greet(partner_id, graph_index)
    for step in range(1, peers):
        greet(sys_index, lax.rem(graph_index + step, peers))
    greeted = (
        peers + jnp.where(chip < last, 1, 0) + jnp.where(chip > 0, 1, 0)
    )
    pl.semaphore_wait(barrier, greeted)

    def own_piece(j):
        return zero_ref if j == 0 else one_ref.at[j - 1]

    def raw_piece(e, j):
        return raw_zero.at[e] if j == 0 else raw_one.at[e, j - 1]

    def raw_copy(e, j, way, source=None):
        target = (up_id, down_id, partner_id)[way]
        return pltpu.make_async_remote_copy(
            src_ref=raw_piece(e, j) if source is None else source,
            dst_ref=raw_piece(e, j),
            send_sem=raw_send.at[way, e, j],
            recv_sem=raw_recv.at[e, j],
            device_id=(target, graph_index),
            device_id_type=MESH,
        )

    goes_up = chip + 1 <= last - 1
    goes_down = chip - 1 >= 1
    pieces = 1 + HALVES

    def feat_copy(step):
        return pltpu.make_async_remote_copy(
            src_ref=feat_ref,
            dst_ref=feats.at[graph_index],
            send_sem=feat_send.at[step],
            recv_sem=feat_recv.at[step],
            device_id=(sys_index, lax.rem(graph_index + step, peers)),
            device_id_type=MESH,
        )

    for step in range(1, peers):
        feat_copy(step).start()

    def each_own(act):
        for j in range(pieces):

            @pl.when(goes_up)
            def _():
                act(raw_copy(sys_index, j, 0, own_piece(j)))

            @pl.when(goes_down)
            def _():
                act(raw_copy(sys_index, j, 1, own_piece(j)))

            act(raw_copy(sys_index, j, 2, own_piece(j)))

    each_own(lambda copy: copy.start())

    def forward(s, j, sent):
        from_low = jnp.logical_and(chip - 1 - s >= 0, chip <= last - 1)
        low = jnp.maximum(chip - 1 - s, 0) * CORES + core
        from_high = jnp.logical_and(chip + 1 + s <= last, chip >= 1)
        high = jnp.minimum(chip + 1 + s, last) * CORES + core

        @pl.when(from_low)
        def _():
            if not sent:
                raw_copy(low, j, 2).wait_recv()

            @pl.when(goes_up)
            def _():
                copy = raw_copy(low, j, 0)
                copy.wait_send() if sent else copy.start()

            copy = raw_copy(low, j, 2)
            copy.wait_send() if sent else copy.start()

        @pl.when(from_high)
        def _():
            if not sent:
                raw_copy(high, j, 2).wait_recv()

            @pl.when(goes_down)
            def _():
                copy = raw_copy(high, j, 1)
                copy.wait_send() if sent else copy.start()

            copy = raw_copy(high, j, 2)
            copy.wait_send() if sent else copy.start()

    atoms = slot_ref.shape[1]
    edges = near_ref.shape[1]
    frames, harmonics = frame_ref.shape[0], frame_ref.shape[1]
    channels = feat_ref.shape[2]
    zero_rows = zero_ref.shape[0]
    one_rows = one_ref.shape[1]
    side = one_ref.shape[2] // 2

    raw_zero[sys_index] = zero_ref[...]
    raw_one[sys_index] = one_ref[...]
    feats[graph_index] = feat_ref[...]
    padded[...] = jnp.zeros_like(padded)
    for r in range(frames):
        padded[r, :harmonics, :] = frame_ref[r]

    by_id = (
        lax.broadcasted_iota(jnp.int32, (atoms, edges), 0) == near_ref[...]
    ).astype(jnp.bfloat16)
    by_slot = (
        lax.broadcasted_iota(jnp.int32, (atoms, atoms), 0) == slot_ref[...]
    ).astype(jnp.bfloat16)
    chosen[...] = jnp.dot(by_slot, by_id, preferred_element_type=jnp.float32).astype(
        jnp.bfloat16
    )

    for step in range(1, peers):
        feat_copy(step).wait_recv()
    for k in range(harmonics):
        block = feats[:, k].reshape(atoms, channels)
        turned[pl.ds(k * channels, channels), :] = block.T

    band = 16

    def rotate_tile(t, carry):
        lanes = pl.ds(pl.multiple_of(t * LANES, LANES), LANES)
        picked[...] = jnp.dot(
            turned[...], chosen[:, lanes], preferred_element_type=jnp.float32
        ).astype(jnp.bfloat16)
        for r in range(frames):
            rows32[r] = frame_ref[r, :, lanes].astype(jnp.float32)

        def widen(r, carry):
            for k in range(harmonics):
                spread[r, k] = jnp.broadcast_to(
                    rows32[r, k : k + 1, :], (band, LANES)
                ).astype(jnp.bfloat16)
            return carry

        lax.fori_loop(0, frames, widen, 0)

        def rotate_band(b, carry):
            start = pl.multiple_of(b * 2 * band, 2 * band)
            held = [
                [
                    picked[pl.ds(k * channels + start + h * band, band), :]
                    for k in range(harmonics)
                ]
                for h in range(2)
            ]
            for r in range(frames):
                weights = [spread[r, k] for k in range(harmonics)]
                for h in range(2):
                    groups = []
                    for low in range(0, harmonics, 5):
                        part = weights[low] * held[h][low]
                        for k in range(low + 1, min(low + 5, harmonics)):
                            part = part + weights[k] * held[h][k]
                        groups.append(part)
                    rotated[pl.ds(r * channels + start + h * band, band), lanes] = tree_sum(
                        groups
                    )
            return carry

        lax.fori_loop(0, channels // (2 * band), rotate_band, 0)
        tiles = edges // LANES
        for j in range(pieces):

            @pl.when(t == min(tiles - 1, (tiles * (j + 1)) // pieces - 1))
            def _():
                forward(0, j, False)

        return carry

    lax.fori_loop(0, edges // LANES, rotate_tile, 0)

    def wait_partner(j):
        for other in range(chips):
            e = other * CORES + (1 - core)

            @pl.when(jnp.logical_or(is_inner, chip == other))
            def _():
                raw_copy(e, j, 2).wait_recv()

    def weighted(get, put, system, members, rows, extra=None):
        step = band if rows % band == 0 else rows

        def body(i, carry):
            at = pl.ds(pl.multiple_of(i * step, step), step)
            acc = None
            for e in members:
                term = mix_ref[system, e] * get(e, at).astype(jnp.float32)
                acc = term if acc is None else acc + term
            if extra is not None:
                acc = acc + extra(at).astype(jnp.float32)
            put(at, acc.astype(jnp.bfloat16))
            return carry

        lax.fori_loop(0, rows // step, body, 0)

    def getter(j):
        if j == 0:
            return lambda e, at: raw_zero[e, at, :]
        return lambda e, at: raw_one[e, j - 1, at, :]

    rows_of = [zero_rows] + [one_rows] * HALVES

    def part_piece(side_index, j):
        return part_zero.at[side_index] if j == 0 else part_one.at[side_index, j - 1]

    def end_piece(j):
        return end_zero if j == 0 else end_one.at[j - 1]

    def part_copy(side_index, j):
        return pltpu.make_async_remote_copy(
            src_ref=part_piece(side_index, j),
            dst_ref=end_piece(j),
            send_sem=part_send.at[side_index, j],
            recv_sem=part_recv.at[j],
            device_id=((down_id, up_id)[side_index], graph_index),
            device_id_type=MESH,
        )

    def map_piece(g, j):
        return map_zero.at[g] if j == 0 else map_one.at[j - 1, g]

    def map_copy(step, j):
        return pltpu.make_async_remote_copy(
            src_ref=map_piece(graph_index, j),
            dst_ref=map_piece(graph_index, j),
            send_sem=map_send.at[step, j],
            recv_sem=map_recv.at[step, j],
            device_id=(sys_index, lax.rem(graph_index + step, peers)),
            device_id_type=MESH,
        )

    def put_map(j):
        ref = map_piece(graph_index, j)

        def put(at, value):
            ref[at, :] = value

        return put

    def put_part(side_index, j):
        ref = part_piece(side_index, j)

        def put(at, value):
            ref[at, :] = value

        return put

    def merge(j):
        for s in range(1, chips - 2):
            forward(s, j, False)
        wait_partner(j)

        @pl.when(chip == 1)
        def _():
            weighted(
                getter(j), put_part(0, j), core, range(CORES, experts), rows_of[j]
            )
            part_copy(0, j).start()

        @pl.when(chip == last - 1)
        def _():
            weighted(
                getter(j),
                put_part(1, j),
                experts - CORES + core,
                range(experts - CORES),
                rows_of[j],
            )
            part_copy(1, j).start()

        @pl.when(is_inner)
        def _():
            weighted(getter(j), put_map(j), sys_index, range(experts), rows_of[j])

        def finish(members):
            part_copy(0, j).wait_recv()
            ref = end_piece(j)
            weighted(
                getter(j),
                put_map(j),
                sys_index,
                members,
                rows_of[j],
                extra=lambda at: ref[at, :],
            )

        @pl.when(chip == 0)
        def _():
            finish(range(CORES))

        @pl.when(chip == last)
        def _():
            finish(range(experts - CORES, experts))

        for step in range(1, peers):
            map_copy(step, j).start()

    def wait_maps(j):
        for step in range(1, peers):
            map_copy(step, j).wait_recv()

    order_zero = (LMAX + 1) * channels
    cuts = [(at, min(WIDE, edges - at)) for at in range(0, edges, WIDE)]

    def apply_zero():
        wait_maps(0)
        for at, width in cuts:
            value = rotated[:order_zero, at : at + width]
            gate = gate_ref[:, at : at + width]
            for g in range(peers):
                y = jnp.dot(map_zero[g], value, preferred_element_type=jnp.float32)
                message[g * zero_rows : (g + 1) * zero_rows, at : at + width] = (
                    gate * y
                ).astype(jnp.bfloat16)

    def apply_one(h):
        wait_maps(1 + h)
        for g in range(peers):
            real = map_one[h, g, :, :side]
            imag = map_one[h, g, :, side:]
            base = 2 * g * one_rows
            stacked[base : base + one_rows, :side] = real
            stacked[base : base + one_rows, side:] = -imag
            stacked[base + one_rows : base + 2 * one_rows, :side] = imag
            stacked[base + one_rows : base + 2 * one_rows, side:] = real
        for at, width in cuts:
            y = jnp.dot(
                stacked[...],
                rotated[order_zero:, at : at + width],
                preferred_element_type=jnp.float32,
            )
            y = (gate_ref[:, at : at + width] * y).astype(jnp.bfloat16)
            for g in range(peers):
                base = 2 * g * one_rows
                to = order_zero + (g * HALVES + h) * one_rows
                message[to : to + one_rows, at : at + width] = y[base : base + one_rows]
                to = to + side
                message[to : to + one_rows, at : at + width] = y[
                    base + one_rows : base + 2 * one_rows
                ]

    merge(0)
    merge(1)
    apply_zero()
    for h in range(1, HALVES):
        merge(1 + h)
        apply_one(h - 1)
    apply_one(HALVES - 1)

    deep = padded.shape[1]
    total[...] = jnp.zeros_like(total)
    for at, width in cuts:
        first = at // NEIGH
        final = (at + width - 1) // NEIGH
        owner = lax.broadcasted_iota(jnp.int32, (deep, width), 1) + at
        masks = [
            jnp.logical_and(owner >= a * NEIGH, owner < (a + 1) * NEIGH)
            for a in range(first, final + 1)
        ]
        columns = []
        for r in range(frames):
            rows = padded[r, :, at : at + width]
            columns.append(
                jnp.concatenate(
                    [jnp.where(mask, rows, jnp.zeros_like(rows)) for mask in masks], axis=0
                )
            )
        left = jnp.concatenate(columns, axis=1)
        right = jnp.concatenate(
            [
                message[r * channels : (r + 1) * channels, at : at + width]
                for r in range(frames)
            ],
            axis=1,
        )
        total[first * deep : (final + 1) * deep, :] += lax.dot_general(
            left, right, (((1,), (1,)), ((), ())), preferred_element_type=jnp.float32
        )
    scale = 1.0 / math.sqrt(NEIGH)
    for a in range(edges // NEIGH):
        out_ref[a] = (total[a * deep : a * deep + harmonics, :] * scale).astype(jnp.bfloat16)

    for step in range(1, peers):
        feat_copy(step).wait_send()
    each_own(lambda copy: copy.wait_send())
    for j in range(pieces):
        for s in range(0, chips - 2):
            forward(s, j, True)

        @pl.when(chip == 1)
        def _():
            part_copy(0, j).wait_send()

        @pl.when(chip == last - 1)
        def _():
            part_copy(1, j).wait_send()

        for step in range(1, peers):
            map_copy(step, j).wait_send()


def shards(
    systems,
    peers,
    node_features,
    atom_slot,
    neighbour,
    pad_mask,
    envelope,
    wigner_rows,
    mix_table,
    zero_weight,
    one_weight,
):
    chips = systems // CORES
    frames, harmonics, edges = wigner_rows.shape[1:]
    own_atoms, _, channels = node_features.shape[1:]
    zero_rows, zero_width = zero_weight.shape[1:]
    one_rows, _, side = one_weight.shape[1:]
    half = one_rows // HALVES
    deep = -(-harmonics // 16) * 16
    bf16, f32 = jnp.bfloat16, jnp.float32
    pieces = 1 + HALVES
    gate = envelope * pad_mask.astype(f32)
    vmem = pl.BlockSpec(memory_space=pltpu.VMEM)
    atoms = atom_slot.shape[1]
    update = pl.pallas_call(
        functools.partial(kernel, chips, peers),
        out_shape=jax.ShapeDtypeStruct((own_atoms, harmonics, channels), bf16),
        in_specs=[vmem] * 5 + [pl.BlockSpec(memory_space=pltpu.SMEM)] + [vmem] * 2,
        out_specs=vmem,
        scratch_shapes=[
            pltpu.VMEM((peers, harmonics, own_atoms, channels), bf16),
            pltpu.VMEM((harmonics * channels, atoms), bf16),
            pltpu.VMEM((atoms, edges), bf16),
            pltpu.VMEM((harmonics * channels, LANES), bf16),
            pltpu.VMEM((frames, harmonics, LANES), f32),
            pltpu.VMEM((frames, harmonics, 16, LANES), bf16),
            pltpu.VMEM((frames * channels, edges), bf16),
            pltpu.VMEM((frames * channels, edges), bf16),
            pltpu.VMEM((frames, deep, edges), bf16),
            pltpu.VMEM((systems, zero_rows, zero_width), bf16),
            pltpu.VMEM((systems, HALVES, half, 2 * side), bf16),
            pltpu.VMEM((2, zero_rows, zero_width), bf16),
            pltpu.VMEM((2, HALVES, half, 2 * side), bf16),
            pltpu.VMEM((zero_rows, zero_width), bf16),
            pltpu.VMEM((HALVES, half, 2 * side), bf16),
            pltpu.VMEM((peers, zero_rows, zero_width), bf16),
            pltpu.VMEM((HALVES, peers, half, 2 * side), bf16),
            pltpu.VMEM((2 * peers * half, 2 * side), bf16),
            pltpu.VMEM((own_atoms * deep, channels), f32),
            pltpu.SemaphoreType.DMA((3, systems, pieces)),
            pltpu.SemaphoreType.DMA((systems, pieces)),
            pltpu.SemaphoreType.DMA((2, pieces)),
            pltpu.SemaphoreType.DMA((pieces,)),
            pltpu.SemaphoreType.DMA((peers,)),
            pltpu.SemaphoreType.DMA((peers,)),
            pltpu.SemaphoreType.DMA((peers, pieces)),
            pltpu.SemaphoreType.DMA((peers, pieces)),
        ],
        compiler_params=pltpu.CompilerParams(
            collective_id=0, has_side_effects=True, vmem_limit_bytes=60 * 1024 * 1024
        ),
        name="edge_convolution",
    )(
        jnp.transpose(node_features[0], (1, 0, 2)),
        atom_slot,
        neighbour,
        gate,
        wigner_rows[0],
        mix_table,
        zero_weight[0],
        one_weight[0].reshape(HALVES, half, 2 * side),
    )
    return update[None]


def solution(mesh):
    return jax.shard_map(
        functools.partial(shards, mesh.shape["sys"], mesh.shape["graph"]),
        mesh=mesh,
        in_specs=(
            P("sys", "graph", None, None),
            P("sys", None),
            P("sys", "graph"),
            P("sys", "graph"),
            P("sys", "graph"),
            P("sys", None, None, "graph"),
            P(),
            P("sys", "graph", None),
            P("sys", "graph", None, None),
        ),
        out_specs=P("sys", "graph", None, None),
        check_vma=False,
    )
```

```python
import functools
import math

import jax
import jax.numpy as jnp
from jax import lax
from jax.experimental import pallas as pl
from jax.experimental.pallas import tpu as pltpu
from jax.sharding import PartitionSpec as P

LMAX = 4
NEIGH = 72
CORES = 2
LANES = 128
WIDE = 256
ZERO_PARTS = 2
ONE_PARTS = 4
MESH = pl.DeviceIdType.MESH


def tree_sum(terms):
    while len(terms) > 1:
        terms = [
            terms[i] + terms[i + 1] if i + 1 < len(terms) else terms[i]
            for i in range(0, len(terms), 2)
        ]
    return terms[0]


def kernel(
    chips,
    peers,
    feat_ref,
    slot_ref,
    near_ref,
    mask_ref,
    envelope_ref,
    frame_ref,
    mix_ref,
    zero_ref,
    one_ref,
    out_ref,
    feats,
    turned,
    chosen,
    pair,
    gate_ref,
    picked,
    rows32,
    spread,
    rotated,
    message,
    padded,
    raw_zero,
    raw_one,
    part_zero,
    part_one,
    end_zero,
    end_one,
    map_zero,
    map_one,
    stacked,
    total,
    raw_send,
    raw_recv,
    part_send,
    part_recv,
    feat_send,
    feat_recv,
    map_send,
    map_recv,
):
    experts = chips * CORES
    sys_index = lax.axis_index("sys")
    graph_index = lax.axis_index("graph")
    chip = sys_index // CORES
    core = sys_index % CORES
    up_id = jnp.minimum(sys_index + CORES, experts - 1)
    down_id = jnp.maximum(sys_index - CORES, 0)
    partner_id = chip * CORES + (1 - core)
    last = chips - 1
    is_inner = jnp.logical_and(chip > 0, chip < last)
    is_end = jnp.logical_or(chip == 0, chip == last)

    barrier = pltpu.get_barrier_semaphore()

    def greet(target_sys, target_graph):
        pl.semaphore_signal(
            barrier, inc=1, device_id=(target_sys, target_graph), device_id_type=MESH
        )

    @pl.when(chip < last)
    def _():
        greet(up_id, graph_index)

    @pl.when(chip > 0)
    def _():
        greet(down_id, graph_index)

    greet(partner_id, graph_index)
    for step in range(1, peers):
        greet(sys_index, lax.rem(graph_index + step, peers))
    greeted = (
        peers + jnp.where(chip < last, 1, 0) + jnp.where(chip > 0, 1, 0)
    )
    pl.semaphore_wait(barrier, greeted)

    def own_piece(j):
        return zero_ref.at[j] if j < ZERO_PARTS else raw_piece(sys_index, j)

    def raw_piece(e, j):
        return raw_zero.at[e, j] if j < ZERO_PARTS else raw_one.at[e, j - ZERO_PARTS]

    def raw_copy(e, j, way, source=None):
        target = (up_id, down_id, partner_id)[way]
        return pltpu.make_async_remote_copy(
            src_ref=raw_piece(e, j) if source is None else source,
            dst_ref=raw_piece(e, j),
            send_sem=raw_send.at[way, e, j],
            recv_sem=raw_recv.at[e, j],
            device_id=(target, graph_index),
            device_id_type=MESH,
        )

    goes_up = chip + 1 <= last - 1
    goes_down = chip - 1 >= 1
    pieces = ZERO_PARTS + ONE_PARTS

    def feat_copy(step):
        return pltpu.make_async_remote_copy(
            src_ref=feat_ref,
            dst_ref=feats.at[graph_index],
            send_sem=feat_send.at[step],
            recv_sem=feat_recv.at[step],
            device_id=(sys_index, lax.rem(graph_index + step, peers)),
            device_id_type=MESH,
        )

    for step in range(1, peers):
        feat_copy(step).start()

    def send_own(j, act):
        @pl.when(goes_up)
        def _():
            act(raw_copy(sys_index, j, 0, own_piece(j)))

        @pl.when(goes_down)
        def _():
            act(raw_copy(sys_index, j, 1, own_piece(j)))

        act(raw_copy(sys_index, j, 2, own_piece(j)))

    def start(copy):
        copy.start()

    for j in range(ZERO_PARTS):
        send_own(j, start)

    def forward(s, j, sent):
        from_low = jnp.logical_and(chip - 1 - s >= 0, chip <= last - 1)
        low = jnp.maximum(chip - 1 - s, 0) * CORES + core
        from_high = jnp.logical_and(chip + 1 + s <= last, chip >= 1)
        high = jnp.minimum(chip + 1 + s, last) * CORES + core

        @pl.when(from_low)
        def _():
            if not sent:
                raw_copy(low, j, 2).wait_recv()

            @pl.when(goes_up)
            def _():
                copy = raw_copy(low, j, 0)
                copy.wait_send() if sent else copy.start()

            copy = raw_copy(low, j, 2)
            copy.wait_send() if sent else copy.start()

        @pl.when(from_high)
        def _():
            if not sent:
                raw_copy(high, j, 2).wait_recv()

            @pl.when(goes_down)
            def _():
                copy = raw_copy(high, j, 1)
                copy.wait_send() if sent else copy.start()

            copy = raw_copy(high, j, 2)
            copy.wait_send() if sent else copy.start()

    atoms = slot_ref.shape[1]
    edges = near_ref.shape[1]
    harmonics, frames = frame_ref.shape[0], frame_ref.shape[1]
    channels = feat_ref.shape[2]
    zero_rows = zero_ref.shape[1]
    one_rows = one_ref.shape[0] // ONE_PARTS
    side = one_ref.shape[2]

    pair[...] = one_ref[...].astype(jnp.float32)
    for q in range(ONE_PARTS):
        for part in range(2):
            raw_one[sys_index, q, :, part * side : (part + 1) * side] = pair[
                q * one_rows : (q + 1) * one_rows, part, :
            ].astype(jnp.bfloat16)

    @pl.when(is_end)
    def _():
        for j in range(ZERO_PARTS, pieces):
            send_own(j, start)

    raw_zero[sys_index] = zero_ref[...]
    feats[graph_index] = feat_ref[...]
    gate_ref[...] = envelope_ref[...] * mask_ref[...].astype(jnp.float32)
    padded[...] = jnp.zeros_like(padded)
    by_id = (
        lax.broadcasted_iota(jnp.int32, (atoms, edges), 0) == near_ref[...]
    ).astype(jnp.bfloat16)
    by_slot = (
        lax.broadcasted_iota(jnp.int32, (atoms, atoms), 0) == slot_ref[...]
    ).astype(jnp.bfloat16)
    chosen[...] = jnp.dot(by_slot, by_id, preferred_element_type=jnp.float32).astype(
        jnp.bfloat16
    )

    for step in range(1, peers):
        feat_copy(step).wait_recv()
    for k in range(harmonics):
        block = feats[:, k].reshape(atoms, channels)
        turned[pl.ds(k * channels, channels), :] = block.T

    band = 16

    def rotate_tile(t, carry):
        lanes = pl.ds(pl.multiple_of(t * LANES, LANES), LANES)
        picked[...] = jnp.dot(
            turned[...], chosen[:, lanes], preferred_element_type=jnp.float32
        ).astype(jnp.bfloat16)
        for k in range(harmonics):
            rows32[k] = frame_ref[k, :, lanes].astype(jnp.float32)
        for r in range(frames):
            padded[r, :harmonics, lanes] = rows32[:, r, :].astype(jnp.bfloat16)

        def widen(k, carry):
            for r in range(frames):
                spread[r, k] = jnp.broadcast_to(
                    rows32[k, r : r + 1, :], (band, LANES)
                ).astype(jnp.bfloat16)
            return carry

        lax.fori_loop(0, harmonics, widen, 0)

        def rotate_band(b, carry):
            begin = pl.multiple_of(b * 2 * band, 2 * band)
            held = [
                [
                    picked[pl.ds(k * channels + begin + h * band, band), :]
                    for k in range(harmonics)
                ]
                for h in range(2)
            ]
            for r in range(frames):
                weights = [spread[r, k] for k in range(harmonics)]
                for h in range(2):
                    groups = []
                    for low in range(0, harmonics, 5):
                        part = weights[low] * held[h][low]
                        for k in range(low + 1, min(low + 5, harmonics)):
                            part = part + weights[k] * held[h][k]
                        groups.append(part)
                    rotated[pl.ds(r * channels + begin + h * band, band), lanes] = tree_sum(
                        groups
                    )
            return carry

        lax.fori_loop(0, channels // (2 * band), rotate_band, 0)
        for name, j, tile in plan:

            @pl.when(t == tile)
            def _():
                first_leg(j) if name == "leg" else merge(j)

        return carry

    def wait_partner(j):
        for other in range(chips):
            e = other * CORES + (1 - core)

            @pl.when(jnp.logical_or(is_inner, chip == other))
            def _():
                raw_copy(e, j, 2).wait_recv()

    def weighted(get, put, system, members, rows, extra=None):
        step = band if rows % band == 0 else rows

        def body(i, carry):
            at = pl.ds(pl.multiple_of(i * step, step), step)
            acc = None
            for e in members:
                term = mix_ref[system, e] * get(e, at).astype(jnp.float32)
                acc = term if acc is None else acc + term
            if extra is not None:
                acc = acc + extra(at).astype(jnp.float32)
            put(at, acc.astype(jnp.bfloat16))
            return carry

        lax.fori_loop(0, rows // step, body, 0)

    def getter(j):
        if j < ZERO_PARTS:
            return lambda e, at: raw_zero[e, j, at, :]
        return lambda e, at: raw_one[e, j - ZERO_PARTS, at, :]

    rows_of = [zero_rows] * ZERO_PARTS + [one_rows] * ONE_PARTS

    def part_piece(side_index, j):
        if j < ZERO_PARTS:
            return part_zero.at[side_index, j]
        return part_one.at[side_index, j - ZERO_PARTS]

    def end_piece(j):
        return end_zero.at[j] if j < ZERO_PARTS else end_one.at[j - ZERO_PARTS]

    def part_copy(side_index, j):
        return pltpu.make_async_remote_copy(
            src_ref=part_piece(side_index, j),
            dst_ref=end_piece(j),
            send_sem=part_send.at[side_index, j],
            recv_sem=part_recv.at[j],
            device_id=((down_id, up_id)[side_index], graph_index),
            device_id_type=MESH,
        )

    def map_piece(g, j):
        return map_zero.at[j, g] if j < ZERO_PARTS else map_one.at[j - ZERO_PARTS, g]

    def map_copy(step, j):
        return pltpu.make_async_remote_copy(
            src_ref=map_piece(graph_index, j),
            dst_ref=map_piece(graph_index, j),
            send_sem=map_send.at[step, j],
            recv_sem=map_recv.at[step, j],
            device_id=(sys_index, lax.rem(graph_index + step, peers)),
            device_id_type=MESH,
        )

    def put_map(j):
        ref = map_piece(graph_index, j)

        def put(at, value):
            ref[at, :] = value

        return put

    def put_part(side_index, j):
        ref = part_piece(side_index, j)

        def put(at, value):
            ref[at, :] = value

        return put

    def first_leg(j):
        forward(0, j, False)
        if j + ZERO_PARTS < pieces:

            @pl.when(is_inner)
            def _():
                send_own(j + ZERO_PARTS, start)

    def merge(j):
        for s in range(1, chips - 2):
            forward(s, j, False)
        wait_partner(j)

        @pl.when(chip == 1)
        def _():
            weighted(
                getter(j), put_part(0, j), core, range(CORES, experts), rows_of[j]
            )
            part_copy(0, j).start()

        @pl.when(chip == last - 1)
        def _():
            weighted(
                getter(j),
                put_part(1, j),
                experts - CORES + core,
                range(experts - CORES),
                rows_of[j],
            )
            part_copy(1, j).start()

        @pl.when(is_inner)
        def _():
            weighted(getter(j), put_map(j), sys_index, range(experts), rows_of[j])

        def finish(members):
            part_copy(0, j).wait_recv()
            ref = end_piece(j)
            weighted(
                getter(j),
                put_map(j),
                sys_index,
                members,
                rows_of[j],
                extra=lambda at: ref[at, :],
            )

        @pl.when(chip == 0)
        def _():
            finish(range(CORES))

        @pl.when(chip == last)
        def _():
            finish(range(experts - CORES, experts))

        for step in range(1, peers):
            map_copy(step, j).start()

    def wait_maps(j):
        for step in range(1, peers):
            map_copy(step, j).wait_recv()

    order_zero = (LMAX + 1) * channels
    cuts = [(at, min(WIDE, edges - at)) for at in range(0, edges, WIDE)]

    def apply_zero():
        for j in range(ZERO_PARTS):
            wait_maps(j)
        for at, width in cuts:
            y = jnp.dot(
                map_zero[...].reshape(ZERO_PARTS * peers * zero_rows, order_zero),
                rotated[:order_zero, at : at + width],
                preferred_element_type=jnp.float32,
            )
            y = (gate_ref[:, at : at + width] * y).astype(jnp.bfloat16)
            for j in range(ZERO_PARTS):
                for g in range(peers):
                    base = (j * peers + g) * zero_rows
                    to = (g * ZERO_PARTS + j) * zero_rows
                    message[to : to + zero_rows, at : at + width] = y[base : base + zero_rows]

    group = 2
    whole = group * peers * one_rows

    def apply_one(h):
        for q in range(group):
            wait_maps(ZERO_PARTS + h + q)
            for g in range(peers):
                real = map_one[h + q, g, :, :side]
                imag = map_one[h + q, g, :, side:]
                base = (q * peers + g) * one_rows
                stacked[base : base + one_rows, :side] = real
                stacked[base : base + one_rows, side:] = -imag
                stacked[whole + base : whole + base + one_rows, :side] = imag
                stacked[whole + base : whole + base + one_rows, side:] = real
        for at, width in cuts:
            y = jnp.dot(
                stacked[...],
                rotated[order_zero:, at : at + width],
                preferred_element_type=jnp.float32,
            )
            y = (gate_ref[:, at : at + width] * y).astype(jnp.bfloat16)
            for q in range(group):
                for g in range(peers):
                    base = (q * peers + g) * one_rows
                    to = order_zero + (g * ONE_PARTS + h + q) * one_rows
                    message[to : to + one_rows, at : at + width] = y[base : base + one_rows]
                    to = to + side
                    base = base + whole
                    message[to : to + one_rows, at : at + width] = y[base : base + one_rows]

    tiles = edges // LANES
    order = []
    for j in range(pieces):
        order.append(("leg", j))
        if j >= 1:
            order.append(("merge", j - 1))
    order.append(("merge", pieces - 1))
    late = 2
    plan = [
        (name, j, min(tiles - 1, ((place + 1) * tiles) // (len(order) - late)))
        for place, (name, j) in enumerate(order[:-late])
    ]
    lax.fori_loop(0, tiles, rotate_tile, 0)
    merge(pieces - 2)
    apply_zero()
    merge(pieces - 1)
    for h in range(0, ONE_PARTS, group):
        apply_one(h)

    deep = padded.shape[1]
    total[...] = jnp.zeros_like(total)
    for at, width in cuts:
        first = at // NEIGH
        final = (at + width - 1) // NEIGH
        owner = lax.broadcasted_iota(jnp.int32, (deep, width), 1) + at
        masks = [
            jnp.logical_and(owner >= a * NEIGH, owner < (a + 1) * NEIGH)
            for a in range(first, final + 1)
        ]
        columns = []
        for r in range(frames):
            rows = padded[r, :, at : at + width]
            columns.append(
                jnp.concatenate(
                    [jnp.where(mask, rows, jnp.zeros_like(rows)) for mask in masks], axis=0
                )
            )
        left = jnp.concatenate(columns, axis=1)
        right = jnp.concatenate(
            [
                message[r * channels : (r + 1) * channels, at : at + width]
                for r in range(frames)
            ],
            axis=1,
        )
        product = lax.dot_general(
            left, right, (((1,), (1,)), ((), ())), preferred_element_type=jnp.float32
        )
        total[first : final + 1] += product.reshape(final + 1 - first, deep, channels)
    scale = 1.0 / math.sqrt(NEIGH)
    for k in range(harmonics):
        out_ref[k] = (total[:, k, :] * scale).astype(jnp.bfloat16)

    for step in range(1, peers):
        feat_copy(step).wait_send()
    for j in range(pieces):
        send_own(j, lambda copy: copy.wait_send())
        for s in range(0, chips - 2):
            forward(s, j, True)

        @pl.when(chip == 1)
        def _():
            part_copy(0, j).wait_send()

        @pl.when(chip == last - 1)
        def _():
            part_copy(1, j).wait_send()

        for step in range(1, peers):
            map_copy(step, j).wait_send()


def shards(
    systems,
    peers,
    node_features,
    atom_slot,
    neighbour,
    pad_mask,
    envelope,
    wigner_rows,
    mix_table,
    zero_weight,
    one_weight,
):
    chips = systems // CORES
    frames, harmonics, edges = wigner_rows.shape[1:]
    own_atoms, _, channels = node_features.shape[1:]
    zero_rows, zero_width = zero_weight.shape[1:]
    one_rows, _, side = one_weight.shape[1:]
    half = one_rows // ONE_PARTS
    share = zero_rows // ZERO_PARTS
    deep = -(-harmonics // 16) * 16
    bf16, f32 = jnp.bfloat16, jnp.float32
    pieces = ZERO_PARTS + ONE_PARTS
    vmem = pl.BlockSpec(memory_space=pltpu.VMEM)
    atoms = atom_slot.shape[1]
    update = pl.pallas_call(
        functools.partial(kernel, chips, peers),
        out_shape=jax.ShapeDtypeStruct((harmonics, own_atoms, channels), bf16),
        in_specs=[vmem] * 6 + [pl.BlockSpec(memory_space=pltpu.SMEM)] + [vmem] * 2,
        out_specs=vmem,
        scratch_shapes=[
            pltpu.VMEM((peers, harmonics, own_atoms, channels), bf16),
            pltpu.VMEM((harmonics * channels, atoms), bf16),
            pltpu.VMEM((atoms, edges), bf16),
            pltpu.VMEM((one_rows, 2, side), f32),
            pltpu.VMEM((1, edges), f32),
            pltpu.VMEM((harmonics * channels, LANES), bf16),
            pltpu.VMEM((harmonics, frames, LANES), f32),
            pltpu.VMEM((frames, harmonics, 16, LANES), bf16),
            pltpu.VMEM((frames * channels, edges), bf16),
            pltpu.VMEM((frames * channels, edges), bf16),
            pltpu.VMEM((frames, deep, edges), bf16),
            pltpu.VMEM((systems, ZERO_PARTS, share, zero_width), bf16),
            pltpu.VMEM((systems, ONE_PARTS, half, 2 * side), bf16),
            pltpu.VMEM((2, ZERO_PARTS, share, zero_width), bf16),
            pltpu.VMEM((2, ONE_PARTS, half, 2 * side), bf16),
            pltpu.VMEM((ZERO_PARTS, share, zero_width), bf16),
            pltpu.VMEM((ONE_PARTS, half, 2 * side), bf16),
            pltpu.VMEM((ZERO_PARTS, peers, share, zero_width), bf16),
            pltpu.VMEM((ONE_PARTS, peers, half, 2 * side), bf16),
            pltpu.VMEM((4 * peers * half, 2 * side), bf16),
            pltpu.VMEM((own_atoms, deep, channels), f32),
            pltpu.SemaphoreType.DMA((3, systems, pieces)),
            pltpu.SemaphoreType.DMA((systems, pieces)),
            pltpu.SemaphoreType.DMA((2, pieces)),
            pltpu.SemaphoreType.DMA((pieces,)),
            pltpu.SemaphoreType.DMA((peers,)),
            pltpu.SemaphoreType.DMA((peers,)),
            pltpu.SemaphoreType.DMA((peers, pieces)),
            pltpu.SemaphoreType.DMA((peers, pieces)),
        ],
        compiler_params=pltpu.CompilerParams(
            collective_id=0, has_side_effects=True, vmem_limit_bytes=60 * 1024 * 1024
        ),
        name="edge_convolution",
    )(
        jnp.transpose(node_features[0], (1, 0, 2)),
        atom_slot,
        neighbour,
        pad_mask,
        envelope,
        jnp.transpose(wigner_rows[0], (1, 0, 2)),
        mix_table,
        zero_weight[0].reshape(ZERO_PARTS, share, zero_width),
        one_weight[0],
    )
    return jnp.transpose(update, (1, 0, 2))[None]


def solution(mesh):
    return jax.shard_map(
        functools.partial(shards, mesh.shape["sys"], mesh.shape["graph"]),
        mesh=mesh,
        in_specs=(
            P("sys", "graph", None, None),
            P("sys", None),
            P("sys", "graph"),
            P("sys", "graph"),
            P("sys", "graph"),
            P("sys", None, None, "graph"),
            P(),
            P("sys", "graph", None),
            P("sys", "graph", None, None),
        ),
        out_specs=P("sys", "graph", None, None),
        check_vma=False,
    )
```

```python
import functools
import math

import jax
import jax.numpy as jnp
from jax import lax
from jax.experimental import pallas as pl
from jax.experimental.pallas import tpu as pltpu
from jax.sharding import PartitionSpec as P

LMAX = 4
NEIGH = 72
CORES = 2
LANES = 128
WIDE = 256
ZERO_PARTS = 2
ONE_PARTS = 4
MESH = pl.DeviceIdType.MESH


def tree_sum(terms):
    while len(terms) > 1:
        terms = [
            terms[i] + terms[i + 1] if i + 1 < len(terms) else terms[i]
            for i in range(0, len(terms), 2)
        ]
    return terms[0]


def kernel(
    chips,
    peers,
    feat_ref,
    slot_ref,
    near_ref,
    mask_ref,
    envelope_ref,
    frame_ref,
    mix_ref,
    zero_ref,
    one_ref,
    out_ref,
    feats,
    turned,
    chosen,
    pair,
    gate_ref,
    picked,
    rows32,
    spread,
    rotated,
    message,
    padded,
    raw_zero,
    raw_one,
    part_zero,
    part_one,
    end_zero,
    end_one,
    map_zero,
    map_one,
    stacked,
    total,
    raw_send,
    raw_recv,
    part_send,
    part_recv,
    feat_send,
    feat_recv,
    map_send,
    map_recv,
):
    experts = chips * CORES
    sys_index = lax.axis_index("sys")
    graph_index = lax.axis_index("graph")
    chip = sys_index // CORES
    core = sys_index % CORES
    up_id = jnp.minimum(sys_index + CORES, experts - 1)
    down_id = jnp.maximum(sys_index - CORES, 0)
    partner_id = chip * CORES + (1 - core)
    last = chips - 1
    is_inner = jnp.logical_and(chip > 0, chip < last)
    is_end = jnp.logical_or(chip == 0, chip == last)

    barrier = pltpu.get_barrier_semaphore()

    def greet(target_sys, target_graph):
        pl.semaphore_signal(
            barrier, inc=1, device_id=(target_sys, target_graph), device_id_type=MESH
        )

    @pl.when(chip < last)
    def _():
        greet(up_id, graph_index)

    @pl.when(chip > 0)
    def _():
        greet(down_id, graph_index)

    greet(partner_id, graph_index)
    for step in range(1, peers):
        greet(sys_index, lax.rem(graph_index + step, peers))
    greeted = (
        peers + jnp.where(chip < last, 1, 0) + jnp.where(chip > 0, 1, 0)
    )
    pl.semaphore_wait(barrier, greeted)

    def own_piece(j):
        return zero_ref.at[j] if j < ZERO_PARTS else raw_piece(sys_index, j)

    def raw_piece(e, j):
        return raw_zero.at[e, j] if j < ZERO_PARTS else raw_one.at[e, j - ZERO_PARTS]

    def raw_copy(e, j, way, source=None):
        target = (up_id, down_id, partner_id)[way]
        return pltpu.make_async_remote_copy(
            src_ref=raw_piece(e, j) if source is None else source,
            dst_ref=raw_piece(e, j),
            send_sem=raw_send.at[way, e, j],
            recv_sem=raw_recv.at[e, j],
            device_id=(target, graph_index),
            device_id_type=MESH,
        )

    goes_up = chip + 1 <= last - 1
    goes_down = chip - 1 >= 1
    pieces = ZERO_PARTS + ONE_PARTS

    def feat_copy(step):
        return pltpu.make_async_remote_copy(
            src_ref=feat_ref,
            dst_ref=feats.at[graph_index],
            send_sem=feat_send.at[step],
            recv_sem=feat_recv.at[step],
            device_id=(sys_index, lax.rem(graph_index + step, peers)),
            device_id_type=MESH,
        )

    for step in range(1, peers):
        feat_copy(step).start()

    def send_own(j, act):
        @pl.when(goes_up)
        def _():
            act(raw_copy(sys_index, j, 0, own_piece(j)))

        @pl.when(goes_down)
        def _():
            act(raw_copy(sys_index, j, 1, own_piece(j)))

        act(raw_copy(sys_index, j, 2, own_piece(j)))

    def start(copy):
        copy.start()

    for j in range(ZERO_PARTS):
        send_own(j, start)

    def forward(s, j, sent):
        from_low = jnp.logical_and(chip - 1 - s >= 0, chip <= last - 1)
        low = jnp.maximum(chip - 1 - s, 0) * CORES + core
        from_high = jnp.logical_and(chip + 1 + s <= last, chip >= 1)
        high = jnp.minimum(chip + 1 + s, last) * CORES + core

        @pl.when(from_low)
        def _():
            if not sent:
                raw_copy(low, j, 2).wait_recv()

            @pl.when(goes_up)
            def _():
                copy = raw_copy(low, j, 0)
                copy.wait_send() if sent else copy.start()

            copy = raw_copy(low, j, 2)
            copy.wait_send() if sent else copy.start()

        @pl.when(from_high)
        def _():
            if not sent:
                raw_copy(high, j, 2).wait_recv()

            @pl.when(goes_down)
            def _():
                copy = raw_copy(high, j, 1)
                copy.wait_send() if sent else copy.start()

            copy = raw_copy(high, j, 2)
            copy.wait_send() if sent else copy.start()

    atoms = slot_ref.shape[1]
    edges = near_ref.shape[1]
    harmonics, frames = frame_ref.shape[0], frame_ref.shape[1]
    channels = feat_ref.shape[2]
    zero_rows = zero_ref.shape[1]
    one_rows = one_ref.shape[0] // ONE_PARTS
    side = one_ref.shape[2]

    pair[...] = one_ref[...].astype(jnp.float32)
    for q in range(ONE_PARTS):
        for part in range(2):
            raw_one[sys_index, q, :, part * side : (part + 1) * side] = pair[
                q * one_rows : (q + 1) * one_rows, part, :
            ].astype(jnp.bfloat16)

    @pl.when(is_end)
    def _():
        for j in range(ZERO_PARTS, pieces):
            send_own(j, start)

    raw_zero[sys_index] = zero_ref[...]
    feats[graph_index] = feat_ref[...]
    gate_ref[...] = envelope_ref[...] * mask_ref[...].astype(jnp.float32)
    padded[...] = jnp.zeros_like(padded)
    by_id = (
        lax.broadcasted_iota(jnp.int32, (atoms, edges), 0) == near_ref[...]
    ).astype(jnp.bfloat16)
    by_slot = (
        lax.broadcasted_iota(jnp.int32, (atoms, atoms), 0) == slot_ref[...]
    ).astype(jnp.bfloat16)
    chosen[...] = jnp.dot(by_slot, by_id, preferred_element_type=jnp.float32).astype(
        jnp.bfloat16
    )

    for step in range(1, peers):
        feat_copy(step).wait_recv()
    for k in range(harmonics):
        block = feats[:, k].reshape(atoms, channels)
        turned[pl.ds(k * channels, channels), :] = block.T

    band = 16

    def rotate_tile(t, carry):
        lanes = pl.ds(pl.multiple_of(t * LANES, LANES), LANES)
        picked[...] = jnp.dot(
            turned[...], chosen[:, lanes], preferred_element_type=jnp.float32
        ).astype(jnp.bfloat16)
        for k in range(harmonics):
            rows32[k] = frame_ref[k, :, lanes].astype(jnp.float32)
        for r in range(frames):
            padded[r, :harmonics, lanes] = rows32[:, r, :].astype(jnp.bfloat16)

        def widen(k, carry):
            for r in range(frames):
                spread[r, k] = jnp.broadcast_to(
                    rows32[k, r : r + 1, :], (band, LANES)
                ).astype(jnp.bfloat16)
            return carry

        lax.fori_loop(0, harmonics, widen, 0)

        def rotate_band(b, carry):
            begin = pl.multiple_of(b * 2 * band, 2 * band)
            held = [
                [
                    picked[pl.ds(k * channels + begin + h * band, band), :]
                    for k in range(harmonics)
                ]
                for h in range(2)
            ]
            for r in range(frames):
                weights = [spread[r, k] for k in range(harmonics)]
                for h in range(2):
                    groups = []
                    for low in range(0, harmonics, 5):
                        part = weights[low] * held[h][low]
                        for k in range(low + 1, min(low + 5, harmonics)):
                            part = part + weights[k] * held[h][k]
                        groups.append(part)
                    rotated[pl.ds(r * channels + begin + h * band, band), lanes] = tree_sum(
                        groups
                    )
            return carry

        lax.fori_loop(0, channels // (2 * band), rotate_band, 0)
        for name, j, tile in plan:

            @pl.when(t == tile)
            def _():
                if name == "leg":
                    first_leg(j)
                else:
                    merge_on(is_inner, j)
                    if j >= 1:
                        merge_on(is_end, j - 1)

        return carry

    def wait_partner(j):
        for other in range(chips):
            e = other * CORES + (1 - core)

            @pl.when(jnp.logical_or(is_inner, chip == other))
            def _():
                raw_copy(e, j, 2).wait_recv()

    def weighted(get, put, system, members, rows, extra=None):
        step = band if rows % band == 0 else rows

        def body(i, carry):
            at = pl.ds(pl.multiple_of(i * step, step), step)
            acc = None
            for e in members:
                term = mix_ref[system, e] * get(e, at).astype(jnp.float32)
                acc = term if acc is None else acc + term
            if extra is not None:
                acc = acc + extra(at).astype(jnp.float32)
            put(at, acc.astype(jnp.bfloat16))
            return carry

        lax.fori_loop(0, rows // step, body, 0)

    def getter(j):
        if j < ZERO_PARTS:
            return lambda e, at: raw_zero[e, j, at, :]
        return lambda e, at: raw_one[e, j - ZERO_PARTS, at, :]

    rows_of = [zero_rows] * ZERO_PARTS + [one_rows] * ONE_PARTS

    def part_piece(side_index, j):
        if j < ZERO_PARTS:
            return part_zero.at[side_index, j]
        return part_one.at[side_index, j - ZERO_PARTS]

    def end_piece(j):
        return end_zero.at[j] if j < ZERO_PARTS else end_one.at[j - ZERO_PARTS]

    def part_copy(side_index, j):
        return pltpu.make_async_remote_copy(
            src_ref=part_piece(side_index, j),
            dst_ref=end_piece(j),
            send_sem=part_send.at[side_index, j],
            recv_sem=part_recv.at[j],
            device_id=((down_id, up_id)[side_index], graph_index),
            device_id_type=MESH,
        )

    def map_piece(g, j):
        return map_zero.at[j, g] if j < ZERO_PARTS else map_one.at[j - ZERO_PARTS, g]

    def map_copy(step, j):
        return pltpu.make_async_remote_copy(
            src_ref=map_piece(graph_index, j),
            dst_ref=map_piece(graph_index, j),
            send_sem=map_send.at[step, j],
            recv_sem=map_recv.at[step, j],
            device_id=(sys_index, lax.rem(graph_index + step, peers)),
            device_id_type=MESH,
        )

    def put_map(j):
        ref = map_piece(graph_index, j)

        def put(at, value):
            ref[at, :] = value

        return put

    def put_part(side_index, j):
        ref = part_piece(side_index, j)

        def put(at, value):
            ref[at, :] = value

        return put

    def first_leg(j):
        forward(0, j, False)
        if j + ZERO_PARTS < pieces:

            @pl.when(is_inner)
            def _():
                send_own(j + ZERO_PARTS, start)

    def merge(j):
        for s in range(1, chips - 2):
            forward(s, j, False)
        wait_partner(j)

        @pl.when(chip == 1)
        def _():
            weighted(
                getter(j), put_part(0, j), core, range(CORES, experts), rows_of[j]
            )
            part_copy(0, j).start()

        @pl.when(chip == last - 1)
        def _():
            weighted(
                getter(j),
                put_part(1, j),
                experts - CORES + core,
                range(experts - CORES),
                rows_of[j],
            )
            part_copy(1, j).start()

        @pl.when(is_inner)
        def _():
            weighted(getter(j), put_map(j), sys_index, range(experts), rows_of[j])

        def finish(members):
            part_copy(0, j).wait_recv()
            ref = end_piece(j)
            weighted(
                getter(j),
                put_map(j),
                sys_index,
                members,
                rows_of[j],
                extra=lambda at: ref[at, :],
            )

        @pl.when(chip == 0)
        def _():
            finish(range(CORES))

        @pl.when(chip == last)
        def _():
            finish(range(experts - CORES, experts))

        for step in range(1, peers):
            map_copy(step, j).start()

    def merge_on(flag, j):
        @pl.when(flag)
        def _():
            merge(j)

    def wait_maps(j):
        for step in range(1, peers):
            map_copy(step, j).wait_recv()

    order_zero = (LMAX + 1) * channels
    cuts = [(at, min(WIDE, edges - at)) for at in range(0, edges, WIDE)]

    def apply_zero():
        for j in range(ZERO_PARTS):
            wait_maps(j)
        for at, width in cuts:
            y = jnp.dot(
                map_zero[...].reshape(ZERO_PARTS * peers * zero_rows, order_zero),
                rotated[:order_zero, at : at + width],
                preferred_element_type=jnp.float32,
            )
            y = (gate_ref[:, at : at + width] * y).astype(jnp.bfloat16)
            for j in range(ZERO_PARTS):
                for g in range(peers):
                    base = (j * peers + g) * zero_rows
                    to = (g * ZERO_PARTS + j) * zero_rows
                    message[to : to + zero_rows, at : at + width] = y[base : base + zero_rows]

    group = 2
    whole = group * peers * one_rows

    def apply_one(h):
        for q in range(group):
            wait_maps(ZERO_PARTS + h + q)
            for g in range(peers):
                real = map_one[h + q, g, :, :side]
                imag = map_one[h + q, g, :, side:]
                base = (q * peers + g) * one_rows
                stacked[base : base + one_rows, :side] = real
                stacked[base : base + one_rows, side:] = -imag
                stacked[whole + base : whole + base + one_rows, :side] = imag
                stacked[whole + base : whole + base + one_rows, side:] = real
        for at, width in cuts:
            y = jnp.dot(
                stacked[...],
                rotated[order_zero:, at : at + width],
                preferred_element_type=jnp.float32,
            )
            y = (gate_ref[:, at : at + width] * y).astype(jnp.bfloat16)
            for q in range(group):
                for g in range(peers):
                    base = (q * peers + g) * one_rows
                    to = order_zero + (g * ONE_PARTS + h + q) * one_rows
                    message[to : to + one_rows, at : at + width] = y[base : base + one_rows]
                    to = to + side
                    base = base + whole
                    message[to : to + one_rows, at : at + width] = y[base : base + one_rows]

    tiles = edges // LANES
    order = []
    for j in range(pieces):
        order.append(("leg", j))
        if j >= 1:
            order.append(("merge", j - 1))
    order.append(("merge", pieces - 1))
    late = 2
    plan = [
        (name, j, min(tiles - 1, ((place + 1) * tiles) // (len(order) - late)))
        for place, (name, j) in enumerate(order[:-late])
    ]
    lax.fori_loop(0, tiles, rotate_tile, 0)
    merge_on(is_end, pieces - late - 1)
    merge(pieces - 2)
    apply_zero()
    merge(pieces - 1)
    for h in range(0, ONE_PARTS, group):
        apply_one(h)

    deep = padded.shape[1]
    total[...] = jnp.zeros_like(total)
    for at, width in cuts:
        first = at // NEIGH
        final = (at + width - 1) // NEIGH
        owner = lax.broadcasted_iota(jnp.int32, (deep, width), 1) + at
        masks = [
            jnp.logical_and(owner >= a * NEIGH, owner < (a + 1) * NEIGH)
            for a in range(first, final + 1)
        ]
        columns = []
        for r in range(frames):
            rows = padded[r, :, at : at + width]
            columns.append(
                jnp.concatenate(
                    [jnp.where(mask, rows, jnp.zeros_like(rows)) for mask in masks], axis=0
                )
            )
        left = jnp.concatenate(columns, axis=1)
        right = jnp.concatenate(
            [
                message[r * channels : (r + 1) * channels, at : at + width]
                for r in range(frames)
            ],
            axis=1,
        )
        product = lax.dot_general(
            left, right, (((1,), (1,)), ((), ())), preferred_element_type=jnp.float32
        )
        total[first : final + 1] += product.reshape(final + 1 - first, deep, channels)
    scale = 1.0 / math.sqrt(NEIGH)
    for k in range(harmonics):
        out_ref[k] = (total[:, k, :] * scale).astype(jnp.bfloat16)

    for step in range(1, peers):
        feat_copy(step).wait_send()
    for j in range(pieces):
        send_own(j, lambda copy: copy.wait_send())
        for s in range(0, chips - 2):
            forward(s, j, True)

        @pl.when(chip == 1)
        def _():
            part_copy(0, j).wait_send()

        @pl.when(chip == last - 1)
        def _():
            part_copy(1, j).wait_send()

        for step in range(1, peers):
            map_copy(step, j).wait_send()


def shards(
    systems,
    peers,
    node_features,
    atom_slot,
    neighbour,
    pad_mask,
    envelope,
    wigner_rows,
    mix_table,
    zero_weight,
    one_weight,
):
    chips = systems // CORES
    frames, harmonics, edges = wigner_rows.shape[1:]
    own_atoms, _, channels = node_features.shape[1:]
    zero_rows, zero_width = zero_weight.shape[1:]
    one_rows, _, side = one_weight.shape[1:]
    half = one_rows // ONE_PARTS
    share = zero_rows // ZERO_PARTS
    deep = -(-harmonics // 16) * 16
    bf16, f32 = jnp.bfloat16, jnp.float32
    pieces = ZERO_PARTS + ONE_PARTS
    vmem = pl.BlockSpec(memory_space=pltpu.VMEM)
    atoms = atom_slot.shape[1]
    update = pl.pallas_call(
        functools.partial(kernel, chips, peers),
        out_shape=jax.ShapeDtypeStruct((harmonics, own_atoms, channels), bf16),
        in_specs=[vmem] * 6 + [pl.BlockSpec(memory_space=pltpu.SMEM)] + [vmem] * 2,
        out_specs=vmem,
        scratch_shapes=[
            pltpu.VMEM((peers, harmonics, own_atoms, channels), bf16),
            pltpu.VMEM((harmonics * channels, atoms), bf16),
            pltpu.VMEM((atoms, edges), bf16),
            pltpu.VMEM((one_rows, 2, side), f32),
            pltpu.VMEM((1, edges), f32),
            pltpu.VMEM((harmonics * channels, LANES), bf16),
            pltpu.VMEM((harmonics, frames, LANES), f32),
            pltpu.VMEM((frames, harmonics, 16, LANES), bf16),
            pltpu.VMEM((frames * channels, edges), bf16),
            pltpu.VMEM((frames * channels, edges), bf16),
            pltpu.VMEM((frames, deep, edges), bf16),
            pltpu.VMEM((systems, ZERO_PARTS, share, zero_width), bf16),
            pltpu.VMEM((systems, ONE_PARTS, half, 2 * side), bf16),
            pltpu.VMEM((2, ZERO_PARTS, share, zero_width), bf16),
            pltpu.VMEM((2, ONE_PARTS, half, 2 * side), bf16),
            pltpu.VMEM((ZERO_PARTS, share, zero_width), bf16),
            pltpu.VMEM((ONE_PARTS, half, 2 * side), bf16),
            pltpu.VMEM((ZERO_PARTS, peers, share, zero_width), bf16),
            pltpu.VMEM((ONE_PARTS, peers, half, 2 * side), bf16),
            pltpu.VMEM((4 * peers * half, 2 * side), bf16),
            pltpu.VMEM((own_atoms, deep, channels), f32),
            pltpu.SemaphoreType.DMA((3, systems, pieces)),
            pltpu.SemaphoreType.DMA((systems, pieces)),
            pltpu.SemaphoreType.DMA((2, pieces)),
            pltpu.SemaphoreType.DMA((pieces,)),
            pltpu.SemaphoreType.DMA((peers,)),
            pltpu.SemaphoreType.DMA((peers,)),
            pltpu.SemaphoreType.DMA((peers, pieces)),
            pltpu.SemaphoreType.DMA((peers, pieces)),
        ],
        compiler_params=pltpu.CompilerParams(
            collective_id=0, has_side_effects=True, vmem_limit_bytes=60 * 1024 * 1024
        ),
        name="edge_convolution",
    )(
        jnp.transpose(node_features[0], (1, 0, 2)),
        atom_slot,
        neighbour,
        pad_mask,
        envelope,
        jnp.transpose(wigner_rows[0], (1, 0, 2)),
        mix_table,
        zero_weight[0].reshape(ZERO_PARTS, share, zero_width),
        one_weight[0],
    )
    return jnp.transpose(update, (1, 0, 2))[None]


def solution(mesh):
    return jax.shard_map(
        functools.partial(shards, mesh.shape["sys"], mesh.shape["graph"]),
        mesh=mesh,
        in_specs=(
            P("sys", "graph", None, None),
            P("sys", None),
            P("sys", "graph"),
            P("sys", "graph"),
            P("sys", "graph"),
            P("sys", None, None, "graph"),
            P(),
            P("sys", "graph", None),
            P("sys", "graph", None, None),
        ),
        out_specs=P("sys", "graph", None, None),
        check_vma=False,
    )
```
